32 devices in a mesh: shot: 4 (over y, x), rcv: 8 (over z, core).
Axes of the slice: x: 2, y: 2, z: 4, core: 2. Of those that a mesh axis runs over, the one named last changes fastest.
Arguments:
- modeled: bfloat16 [2, 32, 4, 64, 512], P(None, 'shot', None, 'rcv'), may hold values from -9 to 9
- observed: bfloat16 [2, 4, 32, 64, 512], P(None, 'shot', 'rcv'), may hold values from -60 to 60
- mask: int32 [32, 4, 64], P('shot', None, 'rcv'), may hold values 0 or 1
- shot_order: int32 [32], replicated, may hold values from 0 to 31, as said below
- line_of_slot: int32 [4], replicated, may hold values from 0 to 3, as said below
- coupling: bfloat16 [2, 512, 512], replicated, may hold values from -0.25 to 0.25
- wavelet: float32 [2, 512], replicated, may hold values from -4 to 4
- damping: float32 [512], replicated, may hold values from 2048 to 32768
Outputs:
- new_wavelet: float32 [2, 512], replicated
- residual_out: bfloat16 [2, 32, 4, 64, 512], P(None, 'shot', None, 'rcv')
The draws below stay inside these ranges and needn't reach their ends.
Inputs may be any that keep to these rules, and one draw needn't show every extreme that they name: Group g holds the shots shot_order[g * 8] to shot_order[(g + 1) * 8 - 1]; each shot number appears once. `line_of_slot`: each line appears in exactly one slot.
All inputs are finite; a program needn't handle non-finite values. No bound on the sum of `mask` on one device may be relied on, other than what follows from the above.
Results may differ from the reference program's by a relative error of at most 0.00045.
Values may be sent and summed in bfloat16 or wider, within the bound.
A program may use at most 64 MiB of HBM per device.

```python
import math
import jax
import jax.numpy as jnp
from jax import lax

SG = 8
RB = 8
F = 512
LINES = 4
SHOTS = 32
LINE_R = 64


def build_survey(key):
    base = jax.random.fold_in(key, 811)
    order = jax.random.permutation(jax.random.fold_in(base, 1), SHOTS).astype(jnp.int32)
    slots = jax.random.permutation(jax.random.fold_in(base, 2), LINES).astype(jnp.int32)
    shape = (2, SHOTS, LINES, LINE_R, F)
    traces = jnp.clip(jax.random.normal(jax.random.fold_in(base, 3), shape, jnp.float32), -6.0, 6.0)
    noise_level = 0.3
    traces = traces.astype(jnp.bfloat16).astype(jnp.float32)
    source = jnp.clip(jax.random.normal(jax.random.fold_in(base, 4), (2, F), jnp.float32), -4.0, 4.0)
    group_pos = (jnp.arange(SHOTS) // SG).astype(jnp.float32) / (SHOTS // SG - 1)
    piece_pos = (jnp.arange(LINE_R) // RB).astype(jnp.float32) / (LINE_R // RB - 1)
    amplitude = (3.0 ** group_pos)[:, None, None, None] * (3.0 ** piece_pos)[None, None, :, None] / 3.0
    src_re = source[0][None, None, None, :]
    src_im = source[1][None, None, None, :]
    clean_re = amplitude * (src_re * traces[0] - src_im * traces[1])
    clean_im = amplitude * (src_re * traces[1] + src_im * traces[0])
    noise = jax.random.normal(jax.random.fold_in(base, 6), shape, jnp.float32) * noise_level
    grouped = jnp.stack([clean_re, clean_im]) + noise
    natural = jnp.zeros(shape, jnp.float32).at[:, order].set(grouped)
    by_slot = jnp.take(natural, slots, axis=2)
    stored = jnp.clip(jnp.transpose(by_slot, (0, 2, 1, 3, 4)), -60.0, 60.0)
    return (traces, stored)


def draw_modeled(key, part):
    return build_survey(key)[0].astype(jnp.bfloat16)


def draw_observed(key, part):
    return build_survey(key)[1].astype(jnp.bfloat16)


def draw_shot_order(key, part):
    base = jax.random.fold_in(key, 811)
    return jax.random.permutation(jax.random.fold_in(base, 1), SHOTS).astype(jnp.int32)


def draw_line_of_slot(key, part):
    base = jax.random.fold_in(key, 811)
    return jax.random.permutation(jax.random.fold_in(base, 2), LINES).astype(jnp.int32)


def place_ends(drawn, stream_key, least, largest):
    dims = drawn.shape
    place = [jax.random.randint(jax.random.fold_in(stream_key, axis), (), 0, dims[axis]) for axis in range(len(dims))]
    drawn = drawn.at[tuple(place)].set(least)
    longest = dims.index(max(dims))
    place[longest] = (place[longest] + 1) % dims[longest]
    return drawn.at[tuple(place)].set(largest)


def centred(stream_key, dims, scale, most, held_as=jnp.bfloat16):
    return jnp.clip(scale * jax.random.normal(stream_key, dims, jnp.float32), -most, most).astype(held_as)


def setup_inputs(seed: int = 0) -> dict:
    arg_keys = jax.random.split(jax.random.key(seed), 9)
    modeled = draw_modeled(jax.random.fold_in(arg_keys[8], 71), 0)
    observed = draw_observed(jax.random.fold_in(arg_keys[8], 71), 0)
    mask = place_ends((jax.random.randint(arg_keys[2], (SHOTS, LINES, LINE_R), 0, 5) < 4).astype(jnp.int32), jax.random.fold_in(arg_keys[2], 1), 0, 1)
    shot_order = draw_shot_order(jax.random.fold_in(arg_keys[8], 71), 0)
    line_of_slot = draw_line_of_slot(jax.random.fold_in(arg_keys[8], 71), 0)
    coupling = centred(arg_keys[5], (2, F, F), F ** -0.5, 0.25)
    wavelet = centred(arg_keys[6], (2, F), 1.0, 4.0, jnp.float32)
    damping = jnp.clip(jnp.exp(jax.random.uniform(arg_keys[7], (F,), jnp.float32, math.log(2048.0), math.log(32768.0))), 2048.0, 32768.0)
    return {"modeled": modeled, "observed": observed, "mask": mask, "shot_order": shot_order, "line_of_slot": line_of_slot, "coupling": coupling, "wavelet": wavelet, "damping": damping}


def weigh(trace, coupling):
    real_part = jnp.dot(trace[0], coupling[0], preferred_element_type=jnp.float32) - jnp.dot(trace[1], coupling[1], preferred_element_type=jnp.float32)
    imag_part = jnp.dot(trace[0], coupling[1], preferred_element_type=jnp.float32) + jnp.dot(trace[1], coupling[0], preferred_element_type=jnp.float32)
    return real_part, imag_part


def reference(modeled, observed, mask, shot_order, line_of_slot, coupling, wavelet, damping):
    inverse = jnp.zeros((LINES,), jnp.int32).at[line_of_slot].set(jnp.arange(LINES, dtype=jnp.int32))
    live = mask.astype(jnp.float32)

    def fields(line):
        slot = inverse[line]
        obs_line = lax.dynamic_index_in_dim(observed, slot, 1, keepdims=False)
        obs_line = jnp.take(obs_line, shot_order, axis=1)
        mod_line = lax.dynamic_index_in_dim(modeled, line, 2, keepdims=False)
        live_line = lax.dynamic_index_in_dim(live, line, 1, keepdims=False)[..., None]
        wd_re, wd_im = weigh(obs_line, coupling)
        wg_re, wg_im = weigh(mod_line, coupling)
        return wd_re, wd_im, wg_re, wg_im, live_line

    def partials(line):
        wd_re, wd_im, wg_re, wg_im, live_line = fields(line)
        res_re = live_line * (wd_re - (wavelet[0] * wg_re - wavelet[1] * wg_im))
        res_im = live_line * (wd_im - (wavelet[0] * wg_im + wavelet[1] * wg_re))
        num_re = jnp.sum(wg_re * res_re + wg_im * res_im, axis=(0, 1))
        num_im = jnp.sum(wg_re * res_im - wg_im * res_re, axis=(0, 1))
        den = jnp.sum(live_line * (wg_re * wg_re + wg_im * wg_im), axis=(0, 1))
        return jnp.stack([num_re, num_im]), den

    lines = jnp.arange(LINES, dtype=jnp.int32)
    nums, dens = lax.map(partials, lines)
    num = jnp.sum(nums, axis=0)
    den = jnp.sum(dens, axis=0)
    new_wavelet = wavelet + num / (den + damping)[None, :]

    def outputs(line):
        wd_re, wd_im, wg_re, wg_im, live_line = fields(line)
        out_re = live_line * (wd_re - (new_wavelet[0] * wg_re - new_wavelet[1] * wg_im))
        out_im = live_line * (wd_im - (new_wavelet[0] * wg_im + new_wavelet[1] * wg_re))
        return jnp.stack([out_re, out_im]).astype(jnp.bfloat16)

    stacked = lax.map(outputs, lines)
    residual_out = jnp.transpose(stacked, (1, 2, 0, 3, 4))
    return new_wavelet, residual_out
```

```python
import functools

import jax
import jax.numpy as jnp
from jax import lax
from jax.experimental import pallas as pl
from jax.experimental.pallas import tpu as pltpu
from jax.sharding import PartitionSpec as P

MESH = pl.DeviceIdType.MESH
PIECES = 2


def kernel(
    n_shot,
    n_rcv,
    modeled_hbm,
    observed_hbm,
    coupling_hbm,
    mask_ref,
    order_ref,
    slot_ref,
    wavelet_ref,
    damping_ref,
    new_ref,
    out_ref,
    mod,
    coup,
    spread,
    grouped,
    arrived,
    wg,
    wd,
    live,
    num_mine,
    num_rcv,
    num_group,
    num_shot,
    den_mine,
    den_rcv,
    den_group,
    den_shot,
    load_sem,
    own_sem,
    send1,
    recv1,
    send2,
    recv2,
    num_send1,
    num_recv1,
    num_send2,
    num_recv2,
    den_send1,
    den_recv1,
    den_send2,
    den_recv2,
):
    me_s = lax.axis_index("shot")
    me_r = lax.axis_index("rcv")
    size, lines, rows, freqs = modeled_hbm.shape[1:]
    held = observed_hbm.shape[2]
    parts = len(spread)
    width = spread[0].shape[2]

    rcv_peers = [lax.rem(me_r + d, n_rcv) for d in range(1, n_rcv)]
    shot_peers = [lax.rem(me_s + d, n_shot) for d in range(1, n_shot)]

    barrier = pltpu.get_barrier_semaphore()
    for r in rcv_peers:
        pl.semaphore_signal(barrier, inc=1, device_id=(me_s, r), device_id_type=MESH)
    for s in shot_peers:
        pl.semaphore_signal(barrier, inc=1, device_id=(s, me_r), device_id_type=MESH)

    load_mod = pltpu.make_async_copy(modeled_hbm, mod, load_sem.at[0])
    load_coup = pltpu.make_async_copy(coupling_hbm, coup, load_sem.at[1])
    load_mod.start()
    load_coup.start()

    def piece(t, r):
        c, h = divmod(t, parts // 2)
        return observed_hbm.at[
            c, 0, :, pl.ds(pl.multiple_of(r * rows, rows), rows), pl.ds(h * width, width)
        ]

    own = []
    for t in range(parts):
        copy = pltpu.make_async_copy(
            piece(t, me_r), spread[t].at[pl.ds(me_r * held, held)], own_sem.at[t]
        )
        copy.start()
        own.append(copy)

    pl.semaphore_wait(barrier, n_rcv + n_shot - 2)

    def spread_copy(t, d):
        return pltpu.make_async_remote_copy(
            src_ref=piece(t, rcv_peers[d - 1]),
            dst_ref=spread[t].at[pl.ds(me_r * held, held)],
            send_sem=send1.at[t, d - 1],
            recv_sem=recv1.at[t, d - 1],
            device_id=(me_s, rcv_peers[d - 1]),
            device_id_type=MESH,
        )

    def group_copy(t, d):
        return pltpu.make_async_remote_copy(
            src_ref=grouped.at[t, d - 1],
            dst_ref=arrived.at[t, me_s],
            send_sem=send2.at[t, d - 1],
            recv_sem=recv2.at[t, d - 1],
            device_id=(shot_peers[d - 1], me_r),
            device_id_type=MESH,
        )

    def rcv_sum(mine, slots, send, recv, start):
        for d in range(1, n_rcv):
            copy = pltpu.make_async_remote_copy(
                src_ref=mine,
                dst_ref=slots.at[me_r],
                send_sem=send.at[d - 1],
                recv_sem=recv.at[d - 1],
                device_id=(me_s, rcv_peers[d - 1]),
                device_id_type=MESH,
            )
            if start:
                copy.start()
            else:
                copy.wait()

    def shot_sum(mine, slots, send, recv, start):
        for d in range(1, n_shot):
            copy = pltpu.make_async_remote_copy(
                src_ref=mine,
                dst_ref=slots.at[me_s],
                send_sem=send.at[d - 1],
                recv_sem=recv.at[d - 1],
                device_id=(shot_peers[d - 1], me_r),
                device_id_type=MESH,
            )
            if start:
                copy.start()
            else:
                copy.wait()

    def total(slots, count):
        out = slots[0]
        for i in range(1, count):
            out = out + slots[i]
        return out

    for t in range(parts):
        for d in range(1, n_rcv):
            spread_copy(t, d).start()

    eye = (
        lax.broadcasted_iota(jnp.int32, (rows, rows), 0)
        == lax.broadcasted_iota(jnp.int32, (rows, rows), 1)
    )
    for p in range(size):
        for l in range(lines):
            flags = jnp.broadcast_to(mask_ref[p, l : l + 1, :].astype(jnp.float32), (rows, rows))
            column = jnp.sum(jnp.where(eye, flags, 0.0), axis=1, keepdims=True)
            live[p * lines + l] = jnp.broadcast_to(column, (rows, live.shape[2]))

    load_mod.wait()
    load_coup.wait()

    def dot(x, c):
        return jnp.dot(x, c, preferred_element_type=jnp.float32)

    tall = size * lines * rows
    x_re = mod[0].reshape(tall, freqs)
    x_im = mod[1].reshape(tall, freqs)
    wg[0] = (dot(x_re, coup[0]) - dot(x_im, coup[1])).reshape(size * lines, rows, freqs)
    wg[1] = (dot(x_re, coup[1]) + dot(x_im, coup[0])).reshape(size * lines, rows, freqs)

    wide = freqs // live.shape[2]

    def live_of(i):
        flag = live[i]
        return jnp.concatenate([flag] * wide, axis=1)

    den = jnp.zeros((rows, freqs), jnp.float32)
    for i in range(size * lines):
        den = den + live_of(i) * (wg[0, i] * wg[0, i] + wg[1, i] * wg[1, i])
    den_mine[...] = jnp.sum(den, axis=0, keepdims=True)
    den_rcv[me_r] = den_mine[...]
    rcv_sum(den_mine, den_rcv, den_send1, den_recv1, True)

    def multiply(t):
        c, h = divmod(t, parts // 2)
        for d in range(1, n_shot):
            group_copy(t, d).wait_recv()
        x = arrived[t].reshape(n_shot * size * rows, width)
        span = slice(h * width, (h + 1) * width)
        if c == 0:
            re = dot(x, coup[0, span, :]).reshape(n_shot, size * rows, freqs)
            im = dot(x, coup[1, span, :]).reshape(n_shot, size * rows, freqs)
        else:
            re = -dot(x, coup[1, span, :]).reshape(n_shot, size * rows, freqs)
            im = dot(x, coup[0, span, :]).reshape(n_shot, size * rows, freqs)
        if t == 0:
            wd[0] = re
            wd[1] = im
        else:
            wd[0] = wd[0] + re
            wd[1] = wd[1] + im

    for t in range(parts):
        own[t].wait()
        for d in range(1, n_rcv):
            spread_copy(t, d).wait_recv()
        for d in list(range(1, n_shot)) + [0]:
            group = shot_peers[d - 1] if d else me_s
            for p in range(0, size, 2):
                first = order_ref[group * size + p]
                second = order_ref[group * size + p + 1]
                pair = jnp.concatenate([spread[t][first], spread[t][second]], axis=0)
                if d:
                    grouped[t, d - 1, p * rows : (p + 2) * rows, :] = pair
                else:
                    arrived[t, me_s, p * rows : (p + 2) * rows, :] = pair
        for d in range(1, n_shot):
            group_copy(t, d).start()
        if t == parts - 1:
            rcv_sum(den_mine, den_rcv, den_send1, den_recv1, False)
            den_group[...] = total(den_rcv, n_rcv)
            den_shot[me_s] = den_group[...]
            shot_sum(den_group, den_shot, den_send2, den_recv2, True)
        if t > 0:
            multiply(t - 1)
    multiply(parts - 1)

    slot_of = []
    for l in range(lines):
        k = jnp.int32(0)
        for j in range(lines):
            k = jnp.where(slot_ref[j] == l, j, k)
        slot_of.append(k)

    w_re, w_im = wavelet_ref[0:1, :], wavelet_ref[1:2, :]
    num_re = jnp.zeros((rows, freqs), jnp.float32)
    num_im = jnp.zeros((rows, freqs), jnp.float32)
    for l in range(lines):
        for p in range(size):
            i = p * lines + l
            g_re, g_im, flag = wg[0, i], wg[1, i], live_of(i)
            at = slice(p * rows, (p + 1) * rows)
            res_re = flag * (wd[0, slot_of[l], at, :] - (w_re * g_re - w_im * g_im))
            res_im = flag * (wd[1, slot_of[l], at, :] - (w_re * g_im + w_im * g_re))
            num_re = num_re + (g_re * res_re + g_im * res_im)
            num_im = num_im + (g_re * res_im - g_im * res_re)
    num_mine[0:1, :] = jnp.sum(num_re, axis=0, keepdims=True)
    num_mine[1:2, :] = jnp.sum(num_im, axis=0, keepdims=True)
    num_rcv[me_r] = num_mine[...]
    rcv_sum(num_mine, num_rcv, num_send1, num_recv1, True)
    rcv_sum(num_mine, num_rcv, num_send1, num_recv1, False)
    num_group[...] = total(num_rcv, n_rcv)
    num_shot[me_s] = num_group[...]
    shot_sum(num_group, num_shot, num_send2, num_recv2, True)
    shot_sum(den_group, den_shot, den_send2, den_recv2, False)
    shot_sum(num_group, num_shot, num_send2, num_recv2, False)
    scale = total(den_shot, n_shot) + damping_ref[...]
    new = wavelet_ref[...] + total(num_shot, n_shot) / scale
    new_ref[...] = new

    n_re, n_im = new[0:1, :], new[1:2, :]
    for p in range(size):
        for l in range(lines):
            i = p * lines + l
            g_re, g_im, flag = wg[0, i], wg[1, i], live_of(i)
            at = slice(p * rows, (p + 1) * rows)
            out_re = flag * (wd[0, slot_of[l], at, :] - (n_re * g_re - n_im * g_im))
            out_im = flag * (wd[1, slot_of[l], at, :] - (n_re * g_im + n_im * g_re))
            out_ref[0, p, l] = out_re.astype(jnp.bfloat16)
            out_ref[1, p, l] = out_im.astype(jnp.bfloat16)

    for t in range(parts):
        for d in range(1, n_rcv):
            spread_copy(t, d).wait_send()
        for d in range(1, n_shot):
            group_copy(t, d).wait_send()


def solution(mesh):
    n_shot, n_rcv = mesh.shape["shot"], mesh.shape["rcv"]

    def per_device(modeled, observed, mask, shot_order, line_of_slot, coupling, wavelet, damping):
        _, size, lines, rows, freqs = modeled.shape
        shots = shot_order.shape[0]
        parts = 2 * PIECES
        width = freqs // PIECES
        f32, bf16 = jnp.float32, jnp.bfloat16
        dma = pltpu.SemaphoreType.DMA
        any_ = pl.BlockSpec(memory_space=pl.ANY)
        vmem = pl.BlockSpec(memory_space=pltpu.VMEM)
        smem = pl.BlockSpec(memory_space=pltpu.SMEM)
        return pl.pallas_call(
            functools.partial(kernel, n_shot, n_rcv),
            out_shape=(
                jax.ShapeDtypeStruct(wavelet.shape, f32),
                jax.ShapeDtypeStruct(modeled.shape, bf16),
            ),
            in_specs=[any_, any_, any_, vmem, smem, smem, vmem, vmem],
            out_specs=(vmem, vmem),
            scratch_shapes=[
                pltpu.VMEM(modeled.shape, bf16),
                pltpu.VMEM(coupling.shape, bf16),
                [pltpu.VMEM((shots, rows, width), bf16)] * parts,
                pltpu.VMEM((parts, n_shot - 1, size * rows, width), bf16),
                pltpu.VMEM((parts, n_shot, size * rows, width), bf16),
                pltpu.VMEM((2, size * lines, rows, freqs), f32),
                pltpu.VMEM((2, n_shot, size * rows, freqs), f32),
                pltpu.VMEM((size * lines, rows, 128), f32),
                pltpu.VMEM((2, freqs), f32),
                pltpu.VMEM((n_rcv, 2, freqs), f32),
                pltpu.VMEM((2, freqs), f32),
                pltpu.VMEM((n_shot, 2, freqs), f32),
                pltpu.VMEM((1, freqs), f32),
                pltpu.VMEM((n_rcv, 1, freqs), f32),
                pltpu.VMEM((1, freqs), f32),
                pltpu.VMEM((n_shot, 1, freqs), f32),
                dma((2,)),
                dma((parts,)),
                dma((parts, n_rcv - 1)),
                dma((parts, n_rcv - 1)),
                dma((parts, n_shot - 1)),
                dma((parts, n_shot - 1)),
                dma((n_rcv - 1,)),
                dma((n_rcv - 1,)),
                dma((n_shot - 1,)),
                dma((n_shot - 1,)),
                dma((n_rcv - 1,)),
                dma((n_rcv - 1,)),
                dma((n_shot - 1,)),
                dma((n_shot - 1,)),
            ],
            compiler_params=pltpu.CompilerParams(collective_id=0, has_side_effects=True),
        )(modeled, observed, coupling, mask, shot_order, line_of_slot, wavelet, damping[None, :])

    placed = (
        P(None, "shot", None, "rcv", None),
        P(None, "shot", "rcv", None, None),
        P("shot", None, "rcv"),
        P(),
        P(),
        P(),
        P(),
        P(),
    )
    return jax.shard_map(
        per_device,
        mesh=mesh,
        in_specs=placed,
        out_specs=(P(), P(None, "shot", None, "rcv", None)),
        check_vma=False,
    )
```

```python
import functools

import jax
import jax.numpy as jnp
from jax import lax
from jax.experimental import pallas as pl
from jax.experimental.pallas import tpu as pltpu
from jax.sharding import PartitionSpec as P

MESH = pl.DeviceIdType.MESH
HBM = pltpu.MemorySpace.HBM
PIECES = 2


def peers_of(me, n):
    if n & (n - 1):
        return [lax.rem(me + d, n) for d in range(1, n)]
    out = []
    for j in range(1, n):
        peer, bit = me, 1
        while bit < n:
            if j & bit:
                peer = peer + bit * (1 - 2 * lax.rem(me // bit, 2))
            bit *= 2
        out.append(peer)
    return out


def kernel(
    n_shot,
    n_rcv,
    modeled_hbm,
    observed_hbm,
    coupling_hbm,
    mask_hbm,
    order_hbm,
    slot_hbm,
    wavelet_hbm,
    damping_hbm,
    new_ref,
    wg,
    wdl,
    mask_ref,
    order_ref,
    slot_ref,
    wavelet_ref,
    damping_ref,
    mod,
    obs,
    coup,
    spread,
    grouped,
    arrived,
    wd,
    live,
    num_mine,
    num_rcv,
    num_group,
    num_shot,
    den_mine,
    den_rcv,
    den_group,
    den_shot,
    load_sem,
    own_sem,
    send1,
    recv1,
    send2,
    recv2,
    num_send1,
    num_recv1,
    num_send2,
    num_recv2,
    den_send1,
    den_recv1,
    den_send2,
    den_recv2,
):
    me_s = lax.axis_index("shot")
    me_r = lax.axis_index("rcv")
    size, lines, rows, freqs = modeled_hbm.shape[1:]
    held = observed_hbm.shape[2]
    parts = len(spread)
    width = spread[0].shape[2]

    rcv_peers = peers_of(me_r, n_rcv)
    shot_peers = peers_of(me_s, n_shot)

    barrier = pltpu.get_barrier_semaphore()
    for r in rcv_peers:
        pl.semaphore_signal(barrier, inc=1, device_id=(me_s, r), device_id_type=MESH)
    for s in shot_peers:
        pl.semaphore_signal(barrier, inc=1, device_id=(s, me_r), device_id_type=MESH)

    small = [
        pltpu.make_async_copy(src, dst, load_sem.at[2 + i])
        for i, (src, dst) in enumerate(
            (
                (mask_hbm, mask_ref),
                (order_hbm, order_ref),
                (slot_hbm, slot_ref),
                (wavelet_hbm, wavelet_ref),
                (damping_hbm, damping_ref),
            )
        )
    ]
    for copy in small:
        copy.start()
    load_obs = pltpu.make_async_copy(observed_hbm, obs, load_sem.at[7])
    load_obs.start()
    load_mod = pltpu.make_async_copy(modeled_hbm, mod, load_sem.at[0])
    load_coup = pltpu.make_async_copy(coupling_hbm, coup, load_sem.at[1])
    load_mod.start()
    load_coup.start()

    def piece(t, r):
        c, h = divmod(t, parts // 2)
        return obs.at[
            c, 0, :, pl.ds(pl.multiple_of(r * rows, rows), rows), pl.ds(h * width, width)
        ]

    load_obs.wait()
    own = []
    for t in range(parts):
        copy = pltpu.make_async_copy(
            piece(t, me_r), spread[t].at[pl.ds(me_r * held, held)], own_sem.at[t]
        )
        copy.start()
        own.append(copy)

    pl.semaphore_wait(barrier, n_rcv + n_shot - 2)

    def spread_copy(t, d):
        return pltpu.make_async_remote_copy(
            src_ref=piece(t, rcv_peers[d - 1]),
            dst_ref=spread[t].at[pl.ds(me_r * held, held)],
            send_sem=send1.at[t, d - 1],
            recv_sem=recv1.at[t, d - 1],
            device_id=(me_s, rcv_peers[d - 1]),
            device_id_type=MESH,
        )

    def group_copy(t, d):
        return pltpu.make_async_remote_copy(
            src_ref=grouped.at[t, d - 1],
            dst_ref=arrived.at[t, me_s],
            send_sem=send2.at[t, d - 1],
            recv_sem=recv2.at[t, d - 1],
            device_id=(shot_peers[d - 1], me_r),
            device_id_type=MESH,
        )

    def rcv_sum(mine, slots, send, recv, start):
        for d in range(1, n_rcv):
            copy = pltpu.make_async_remote_copy(
                src_ref=mine,
                dst_ref=slots.at[me_r],
                send_sem=send.at[d - 1],
                recv_sem=recv.at[d - 1],
                device_id=(me_s, rcv_peers[d - 1]),
                device_id_type=MESH,
            )
            if start:
                copy.start()
            else:
                copy.wait()

    def shot_sum(mine, slots, send, recv, start):
        for d in range(1, n_shot):
            copy = pltpu.make_async_remote_copy(
                src_ref=mine,
                dst_ref=slots.at[me_s],
                send_sem=send.at[d - 1],
                recv_sem=recv.at[d - 1],
                device_id=(shot_peers[d - 1], me_r),
                device_id_type=MESH,
            )
            if start:
                copy.start()
            else:
                copy.wait()

    def total(slots, count):
        out = slots[0]
        for i in range(1, count):
            out = out + slots[i]
        return out

    for t in range(parts):
        for d in range(1, n_rcv):
            spread_copy(t, d).start()

    for copy in small:
        copy.wait()

    eye = (
        lax.broadcasted_iota(jnp.int32, (rows, rows), 0)
        == lax.broadcasted_iota(jnp.int32, (rows, rows), 1)
    )
    for p in range(size):
        for l in range(lines):
            flags = jnp.broadcast_to(mask_ref[p, l : l + 1, :].astype(jnp.float32), (rows, rows))
            column = jnp.sum(jnp.where(eye, flags, 0.0), axis=1, keepdims=True)
            live[p * lines + l] = jnp.broadcast_to(column, (rows, live.shape[2]))

    load_mod.wait()
    load_coup.wait()

    def dot(x, c):
        return jnp.dot(x, c, preferred_element_type=jnp.float32)

    tall = size * lines * rows
    x_re = mod[0].reshape(tall, freqs)
    x_im = mod[1].reshape(tall, freqs)
    wide = freqs // live.shape[2]

    def live_of(i):
        flag = live[i]
        return jnp.concatenate([flag] * wide, axis=1)

    wg[0] = (dot(x_re, coup[0]) - dot(x_im, coup[1])).reshape(size * lines, rows, freqs)
    wg[1] = (dot(x_re, coup[1]) + dot(x_im, coup[0])).reshape(size * lines, rows, freqs)

    den = jnp.zeros((rows, freqs), jnp.float32)
    for i in range(size * lines):
        flag = live_of(i)
        g_re, g_im = flag * wg[0, i], flag * wg[1, i]
        wg[0, i] = g_re
        wg[1, i] = g_im
        den = den + (g_re * g_re + g_im * g_im)
    den_mine[...] = jnp.sum(den, axis=0, keepdims=True)
    den_rcv[me_r] = den_mine[...]
    rcv_sum(den_mine, den_rcv, den_send1, den_recv1, True)

    def multiply(t):
        c, h = divmod(t, parts // 2)
        for d in range(1, n_shot):
            group_copy(t, d).wait_recv()
        x = arrived[t].reshape(n_shot * size * rows, width)
        span = slice(h * width, (h + 1) * width)
        if c == 0:
            re = dot(x, coup[0, span, :]).reshape(n_shot, size * rows, freqs)
            im = dot(x, coup[1, span, :]).reshape(n_shot, size * rows, freqs)
        else:
            re = -dot(x, coup[1, span, :]).reshape(n_shot, size * rows, freqs)
            im = dot(x, coup[0, span, :]).reshape(n_shot, size * rows, freqs)
        if t == 0:
            wd[0] = re
            wd[1] = im
        else:
            wd[0] = wd[0] + re
            wd[1] = wd[1] + im

    for t in range(parts):
        own[t].wait()
        for d in range(1, n_rcv):
            spread_copy(t, d).wait_recv()
        for d in list(range(1, n_shot)) + [0]:
            group = shot_peers[d - 1] if d else me_s
            for p in range(0, size, 2):
                first = order_ref[group * size + p]
                second = order_ref[group * size + p + 1]
                pair = jnp.concatenate([spread[t][first], spread[t][second]], axis=0)
                if d:
                    grouped[t, d - 1, p * rows : (p + 2) * rows, :] = pair
                else:
                    arrived[t, me_s, p * rows : (p + 2) * rows, :] = pair
        for d in range(1, n_shot):
            group_copy(t, d).start()
        if t == parts - 1:
            rcv_sum(den_mine, den_rcv, den_send1, den_recv1, False)
            den_group[...] = total(den_rcv, n_rcv)
            den_shot[me_s] = den_group[...]
            shot_sum(den_group, den_shot, den_send2, den_recv2, True)
        if t > 0:
            multiply(t - 1)
    multiply(parts - 1)

    slot_of = []
    for l in range(lines):
        k = jnp.int32(0)
        for j in range(lines):
            k = jnp.where(slot_ref[j] == l, j, k)
        slot_of.append(k)

    w_re, w_im = wavelet_ref[0:1, :], wavelet_ref[1:2, :]
    num_re = jnp.zeros((rows, freqs), jnp.float32)
    num_im = jnp.zeros((rows, freqs), jnp.float32)
    for l in range(lines):
        for p in range(size):
            i = p * lines + l
            g_re, g_im, flag = wg[0, i], wg[1, i], live_of(i)
            at = slice(p * rows, (p + 1) * rows)
            d_re = flag * wd[0, slot_of[l], at, :]
            d_im = flag * wd[1, slot_of[l], at, :]
            wdl[0, i] = d_re
            wdl[1, i] = d_im
            res_re = d_re - (w_re * g_re - w_im * g_im)
            res_im = d_im - (w_re * g_im + w_im * g_re)
            num_re = num_re + (g_re * res_re + g_im * res_im)
            num_im = num_im + (g_re * res_im - g_im * res_re)
    num_mine[0:1, :] = jnp.sum(num_re, axis=0, keepdims=True)
    num_mine[1:2, :] = jnp.sum(num_im, axis=0, keepdims=True)
    num_rcv[me_r] = num_mine[...]
    rcv_sum(num_mine, num_rcv, num_send1, num_recv1, True)
    rcv_sum(num_mine, num_rcv, num_send1, num_recv1, False)
    num_group[...] = total(num_rcv, n_rcv)
    num_shot[me_s] = num_group[...]
    shot_sum(num_group, num_shot, num_send2, num_recv2, True)
    shot_sum(den_group, den_shot, den_send2, den_recv2, False)
    shot_sum(num_group, num_shot, num_send2, num_recv2, False)
    scale = total(den_shot, n_shot) + damping_ref[...]
    new = wavelet_ref[...] + total(num_shot, n_shot) / scale
    new_ref[...] = new

    for t in range(parts):
        for d in range(1, n_rcv):
            spread_copy(t, d).wait_send()
        for d in range(1, n_shot):
            group_copy(t, d).wait_send()


def finish(new_ref, wg, wdl, wave_out, out_ref):
    lines = out_ref.shape[2]
    wave_out[...] = new_ref[...]
    n_re, n_im = new_ref[0:1, :], new_ref[1:2, :]
    for i in range(wg.shape[1]):
        g_re, g_im = wg[0, i], wg[1, i]
        p, l = divmod(i, lines)
        out_ref[0, p, l] = (wdl[0, i] - (n_re * g_re - n_im * g_im)).astype(jnp.bfloat16)
        out_ref[1, p, l] = (wdl[1, i] - (n_re * g_im + n_im * g_re)).astype(jnp.bfloat16)


def solution(mesh):
    n_shot, n_rcv = mesh.shape["shot"], mesh.shape["rcv"]

    def per_device(modeled, observed, mask, shot_order, line_of_slot, coupling, wavelet, damping):
        _, size, lines, rows, freqs = modeled.shape
        shots = shot_order.shape[0]
        parts = 2 * PIECES
        width = freqs // PIECES
        f32, bf16 = jnp.float32, jnp.bfloat16
        dma = pltpu.SemaphoreType.DMA
        hbm = pl.BlockSpec(memory_space=HBM)
        vmem = pl.BlockSpec(memory_space=pltpu.VMEM)
        new, wg, wdl = pl.pallas_call(
            functools.partial(kernel, n_shot, n_rcv),
            out_shape=(
                pltpu.VMEM(wavelet.shape, f32),
                pltpu.VMEM((2, size * lines, rows, freqs), f32),
                pltpu.VMEM((2, size * lines, rows, freqs), f32),
            ),
            in_specs=[hbm] * 8,
            out_specs=(vmem, vmem, vmem),
            scratch_shapes=[
                pltpu.VMEM(mask.shape, jnp.int32),
                pltpu.SMEM(shot_order.shape, jnp.int32),
                pltpu.SMEM(line_of_slot.shape, jnp.int32),
                pltpu.VMEM(wavelet.shape, f32),
                pltpu.VMEM((1, freqs), f32),
                pltpu.VMEM(modeled.shape, bf16),
                pltpu.VMEM(observed.shape, bf16),
                pltpu.VMEM(coupling.shape, bf16),
                [pltpu.VMEM((shots, rows, width), bf16)] * parts,
                pltpu.VMEM((parts, n_shot - 1, size * rows, width), bf16),
                pltpu.VMEM((parts, n_shot, size * rows, width), bf16),
                pltpu.VMEM((2, n_shot, size * rows, freqs), f32),
                pltpu.VMEM((size * lines, rows, 128), f32),
                pltpu.VMEM((2, freqs), f32),
                pltpu.VMEM((n_rcv, 2, freqs), f32),
                pltpu.VMEM((2, freqs), f32),
                pltpu.VMEM((n_shot, 2, freqs), f32),
                pltpu.VMEM((1, freqs), f32),
                pltpu.VMEM((n_rcv, 1, freqs), f32),
                pltpu.VMEM((1, freqs), f32),
                pltpu.VMEM((n_shot, 1, freqs), f32),
                dma((8,)),
                dma((parts,)),
                dma((parts, n_rcv - 1)),
                dma((parts, n_rcv - 1)),
                dma((parts, n_shot - 1)),
                dma((parts, n_shot - 1)),
                dma((n_rcv - 1,)),
                dma((n_rcv - 1,)),
                dma((n_shot - 1,)),
                dma((n_shot - 1,)),
                dma((n_rcv - 1,)),
                dma((n_rcv - 1,)),
                dma((n_shot - 1,)),
                dma((n_shot - 1,)),
            ],
            compiler_params=pltpu.CompilerParams(
                collective_id=0,
                has_side_effects=True,
                vmem_limit_bytes=modeled.size * 48 + coupling.size * 8,
            ),
        )(modeled, observed, coupling, mask, shot_order, line_of_slot, wavelet, damping[None, :])
        return pl.pallas_call(
            finish,
            out_shape=(
                jax.ShapeDtypeStruct(wavelet.shape, f32),
                jax.ShapeDtypeStruct(modeled.shape, bf16),
            ),
            in_specs=[vmem] * 3,
            out_specs=(vmem, vmem),
            compiler_params=pltpu.CompilerParams(vmem_limit_bytes=modeled.size * 16 + (1 << 21)),
        )(*(pltpu.with_memory_space_constraint(x, pltpu.VMEM) for x in (new, wg, wdl)))

    placed = (
        P(None, "shot", None, "rcv", None),
        P(None, "shot", "rcv", None, None),
        P("shot", None, "rcv"),
        P(),
        P(),
        P(),
        P(),
        P(),
    )
    return jax.shard_map(
        per_device,
        mesh=mesh,
        in_specs=placed,
        out_specs=(P(), P(None, "shot", None, "rcv", None)),
        check_vma=False,
    )
```

```python
import functools

import jax
import jax.numpy as jnp
from jax import lax
from jax.experimental import pallas as pl
from jax.experimental.pallas import tpu as pltpu
from jax.sharding import PartitionSpec as P

MESH = pl.DeviceIdType.MESH
HBM = pltpu.MemorySpace.HBM
PIECES = 2


def peers_of(me, n):
    if n & (n - 1):
        return [lax.rem(me + d, n) for d in range(1, n)]
    out = []
    for j in range(1, n):
        peer, bit = me, 1
        while bit < n:
            if j & bit:
                peer = peer + bit * (1 - 2 * lax.rem(me // bit, 2))
            bit *= 2
        out.append(peer)
    return out


def kernel(
    n_shot,
    n_rcv,
    modeled_hbm,
    observed_hbm,
    coupling_hbm,
    mask_hbm,
    order_hbm,
    slot_hbm,
    wavelet_hbm,
    damping_hbm,
    new_ref,
    wg,
    wdl,
    mask_ref,
    order_ref,
    slot_ref,
    wavelet_ref,
    damping_ref,
    mod,
    obs,
    coup,
    spread,
    grouped,
    arrived,
    wd,
    live,
    num_mine,
    num_rcv,
    num_group,
    num_shot,
    den_mine,
    den_rcv,
    den_group,
    den_shot,
    load_sem,
    own_sem,
    send1,
    recv1,
    send2,
    recv2,
    num_send1,
    num_recv1,
    num_send2,
    num_recv2,
    den_send1,
    den_recv1,
    den_send2,
    den_recv2,
):
    me_s = lax.axis_index("shot")
    me_r = lax.axis_index("rcv")
    size, lines, rows, freqs = modeled_hbm.shape[1:]
    held = observed_hbm.shape[2]
    parts = len(spread)
    width = spread[0].shape[2]

    rcv_peers = peers_of(me_r, n_rcv)
    shot_peers = peers_of(me_s, n_shot)

    barrier = pltpu.get_barrier_semaphore()
    for r in rcv_peers:
        pl.semaphore_signal(barrier, inc=1, device_id=(me_s, r), device_id_type=MESH)
    for s in shot_peers:
        pl.semaphore_signal(barrier, inc=1, device_id=(s, me_r), device_id_type=MESH)

    small = [
        pltpu.make_async_copy(src, dst, load_sem.at[2 + i])
        for i, (src, dst) in enumerate(
            (
                (mask_hbm, mask_ref),
                (order_hbm, order_ref),
                (slot_hbm, slot_ref),
                (wavelet_hbm, wavelet_ref),
                (damping_hbm, damping_ref),
            )
        )
    ]
    for copy in small:
        copy.start()
    load_obs = pltpu.make_async_copy(observed_hbm, obs, load_sem.at[7])
    load_obs.start()
    load_mod = pltpu.make_async_copy(modeled_hbm, mod, load_sem.at[0])
    load_coup = pltpu.make_async_copy(coupling_hbm, coup, load_sem.at[1])
    load_mod.start()
    load_coup.start()

    def piece(t, r):
        c, h = divmod(t, parts // 2)
        return obs.at[
            c, 0, :, pl.ds(pl.multiple_of(r * rows, rows), rows), pl.ds(h * width, width)
        ]

    load_obs.wait()
    own = []
    for t in range(parts):
        copy = pltpu.make_async_copy(
            piece(t, me_r), spread[t].at[pl.ds(me_r * held, held)], own_sem.at[t]
        )
        copy.start()
        own.append(copy)

    pl.semaphore_wait(barrier, n_rcv + n_shot - 2)

    def spread_copy(t, d):
        return pltpu.make_async_remote_copy(
            src_ref=piece(t, rcv_peers[d - 1]),
            dst_ref=spread[t].at[pl.ds(me_r * held, held)],
            send_sem=send1.at[t, d - 1],
            recv_sem=recv1.at[t, d - 1],
            device_id=(me_s, rcv_peers[d - 1]),
            device_id_type=MESH,
        )

    def group_copy(t, d):
        return pltpu.make_async_remote_copy(
            src_ref=grouped.at[t, d - 1],
            dst_ref=arrived.at[t, me_s],
            send_sem=send2.at[t, d - 1],
            recv_sem=recv2.at[t, d - 1],
            device_id=(shot_peers[d - 1], me_r),
            device_id_type=MESH,
        )

    def rcv_sum(mine, slots, send, recv, start):
        for d in range(1, n_rcv):
            copy = pltpu.make_async_remote_copy(
                src_ref=mine,
                dst_ref=slots.at[me_r],
                send_sem=send.at[d - 1],
                recv_sem=recv.at[d - 1],
                device_id=(me_s, rcv_peers[d - 1]),
                device_id_type=MESH,
            )
            if start:
                copy.start()
            else:
                copy.wait()

    def shot_sum(mine, slots, send, recv, start):
        for d in range(1, n_shot):
            copy = pltpu.make_async_remote_copy(
                src_ref=mine,
                dst_ref=slots.at[me_s],
                send_sem=send.at[d - 1],
                recv_sem=recv.at[d - 1],
                device_id=(shot_peers[d - 1], me_r),
                device_id_type=MESH,
            )
            if start:
                copy.start()
            else:
                copy.wait()

    def total(slots, count):
        out = slots[0]
        for i in range(1, count):
            out = out + slots[i]
        return out

    for t in range(parts):
        for d in range(1, n_rcv):
            spread_copy(t, d).start()

    for copy in small:
        copy.wait()

    eye = (
        lax.broadcasted_iota(jnp.int32, (rows, rows), 0)
        == lax.broadcasted_iota(jnp.int32, (rows, rows), 1)
    )
    for p in range(size):
        for l in range(lines):
            flags = jnp.broadcast_to(mask_ref[p, l : l + 1, :].astype(jnp.float32), (rows, rows))
            column = jnp.sum(jnp.where(eye, flags, 0.0), axis=1, keepdims=True)
            live[p * lines + l] = jnp.broadcast_to(column, (rows, live.shape[2]))

    load_mod.wait()
    load_coup.wait()

    def dot(x, c):
        return jnp.dot(x, c, preferred_element_type=jnp.float32)

    tall = size * lines * rows
    x_re = mod[0].reshape(tall, freqs)
    x_im = mod[1].reshape(tall, freqs)
    wide = freqs // live.shape[2]

    def live_of(i):
        flag = live[i]
        return jnp.concatenate([flag] * wide, axis=1)

    wg[0] = (dot(x_re, coup[0]) - dot(x_im, coup[1])).reshape(size * lines, rows, freqs)
    wg[1] = (dot(x_re, coup[1]) + dot(x_im, coup[0])).reshape(size * lines, rows, freqs)

    den = jnp.zeros((rows, freqs), jnp.float32)
    for i in range(size * lines):
        flag = live_of(i)
        g_re, g_im = flag * wg[0, i], flag * wg[1, i]
        wg[0, i] = g_re
        wg[1, i] = g_im
        den = den + (g_re * g_re + g_im * g_im)
    den_mine[...] = jnp.sum(den, axis=0, keepdims=True)
    den_rcv[me_r] = den_mine[...]
    rcv_sum(den_mine, den_rcv, den_send1, den_recv1, True)

    def multiply(t):
        c, h = divmod(t, parts // 2)
        for d in range(1, n_shot):
            group_copy(t, d).wait_recv()
        x = arrived[t].reshape(n_shot * size * rows, width)
        span = slice(h * width, (h + 1) * width)
        if c == 0:
            re = dot(x, coup[0, span, :]).reshape(n_shot, size * rows, freqs)
            im = dot(x, coup[1, span, :]).reshape(n_shot, size * rows, freqs)
        else:
            re = -dot(x, coup[1, span, :]).reshape(n_shot, size * rows, freqs)
            im = dot(x, coup[0, span, :]).reshape(n_shot, size * rows, freqs)
        if t == 0:
            wd[0] = re
            wd[1] = im
        else:
            wd[0] = wd[0] + re
            wd[1] = wd[1] + im

    for t in range(parts):
        own[t].wait()
        for d in range(1, n_rcv):
            spread_copy(t, d).wait_recv()
        for d in list(range(1, n_shot)) + [0]:
            group = shot_peers[d - 1] if d else me_s
            for p in range(0, size, 2):
                first = order_ref[group * size + p]
                second = order_ref[group * size + p + 1]
                pair = jnp.concatenate([spread[t][first], spread[t][second]], axis=0)
                if d:
                    grouped[t, d - 1, p * rows : (p + 2) * rows, :] = pair
                else:
                    arrived[t, me_s, p * rows : (p + 2) * rows, :] = pair
        for d in range(1, n_shot):
            group_copy(t, d).start()
        if t == parts - 1:
            rcv_sum(den_mine, den_rcv, den_send1, den_recv1, False)
            den_group[...] = total(den_rcv, n_rcv)
            den_shot[me_s] = den_group[...]
            shot_sum(den_group, den_shot, den_send2, den_recv2, True)
        if t > 0:
            multiply(t - 1)
    multiply(parts - 1)

    slot_of = []
    for l in range(lines):
        k = jnp.int32(0)
        for j in range(lines):
            k = jnp.where(slot_ref[j] == l, j, k)
        slot_of.append(k)

    w_re, w_im = wavelet_ref[0:1, :], wavelet_ref[1:2, :]
    num_re = jnp.zeros((rows, freqs), jnp.float32)
    num_im = jnp.zeros((rows, freqs), jnp.float32)
    for l in range(lines):
        for p in range(size):
            i = p * lines + l
            g_re, g_im, flag = wg[0, i], wg[1, i], live_of(i)
            at = slice(p * rows, (p + 1) * rows)
            d_re = flag * wd[0, slot_of[l], at, :]
            d_im = flag * wd[1, slot_of[l], at, :]
            wdl[0, i] = d_re
            wdl[1, i] = d_im
            res_re = d_re - (w_re * g_re - w_im * g_im)
            res_im = d_im - (w_re * g_im + w_im * g_re)
            num_re = num_re + (g_re * res_re + g_im * res_im)
            num_im = num_im + (g_re * res_im - g_im * res_re)
    num_mine[0:1, :] = jnp.sum(num_re, axis=0, keepdims=True)
    num_mine[1:2, :] = jnp.sum(num_im, axis=0, keepdims=True)
    num_rcv[me_r] = num_mine[...]
    rcv_sum(num_mine, num_rcv, num_send1, num_recv1, True)
    rcv_sum(num_mine, num_rcv, num_send1, num_recv1, False)
    num_group[...] = total(num_rcv, n_rcv)
    num_shot[me_s] = num_group[...]
    shot_sum(num_group, num_shot, num_send2, num_recv2, True)
    shot_sum(den_group, den_shot, den_send2, den_recv2, False)
    shot_sum(num_group, num_shot, num_send2, num_recv2, False)
    scale = total(den_shot, n_shot) + damping_ref[...]
    new = wavelet_ref[...] + total(num_shot, n_shot) / scale
    new_ref[...] = new

    for t in range(parts):
        for d in range(1, n_rcv):
            spread_copy(t, d).wait_send()
        for d in range(1, n_shot):
            group_copy(t, d).wait_send()


def finish(new_ref, wg, wdl, wave_out, out_ref):
    lines = out_ref.shape[2]
    wave_out[...] = new_ref[...]
    n_re, n_im = new_ref[0:1, :], new_ref[1:2, :]
    for i in range(wg.shape[1]):
        g_re, g_im = wg[0, i], wg[1, i]
        p, l = divmod(i, lines)
        out_ref[0, p, l] = (wdl[0, i] - (n_re * g_re - n_im * g_im)).astype(jnp.bfloat16)
        out_ref[1, p, l] = (wdl[1, i] - (n_re * g_im + n_im * g_re)).astype(jnp.bfloat16)


def solution(mesh):
    n_shot, n_rcv = mesh.shape["shot"], mesh.shape["rcv"]

    def per_device(modeled, observed, mask, shot_order, line_of_slot, coupling, wavelet, damping):
        _, size, lines, rows, freqs = modeled.shape
        shots = shot_order.shape[0]
        parts = 2 * PIECES
        width = freqs // PIECES
        f32, bf16 = jnp.float32, jnp.bfloat16
        dma = pltpu.SemaphoreType.DMA
        hbm = pl.BlockSpec(memory_space=HBM)
        vmem = pl.BlockSpec(memory_space=pltpu.VMEM)
        new, wg, wdl = pl.pallas_call(
            functools.partial(kernel, n_shot, n_rcv),
            out_shape=(
                pltpu.VMEM(wavelet.shape, f32),
                pltpu.VMEM((2, size * lines, rows, freqs), f32),
                pltpu.VMEM((2, size * lines, rows, freqs), f32),
            ),
            in_specs=[hbm] * 8,
            out_specs=(vmem, vmem, vmem),
            scratch_shapes=[
                pltpu.VMEM(mask.shape, jnp.int32),
                pltpu.SMEM(shot_order.shape, jnp.int32),
                pltpu.SMEM(line_of_slot.shape, jnp.int32),
                pltpu.VMEM(wavelet.shape, f32),
                pltpu.VMEM((1, freqs), f32),
                pltpu.VMEM(modeled.shape, bf16),
                pltpu.VMEM(observed.shape, bf16),
                pltpu.VMEM(coupling.shape, bf16),
                [pltpu.VMEM((shots, rows, width), bf16)] * parts,
                pltpu.VMEM((parts, n_shot - 1, size * rows, width), bf16),
                pltpu.VMEM((parts, n_shot, size * rows, width), bf16),
                pltpu.VMEM((2, n_shot, size * rows, freqs), f32),
                pltpu.VMEM((size * lines, rows, 128), f32),
                pltpu.VMEM((2, freqs), f32),
                pltpu.VMEM((n_rcv, 2, freqs), f32),
                pltpu.VMEM((2, freqs), f32),
                pltpu.VMEM((n_shot, 2, freqs), f32),
                pltpu.VMEM((1, freqs), f32),
                pltpu.VMEM((n_rcv, 1, freqs), f32),
                pltpu.VMEM((1, freqs), f32),
                pltpu.VMEM((n_shot, 1, freqs), f32),
                dma((8,)),
                dma((parts,)),
                dma((parts, n_rcv - 1)),
                dma((parts, n_rcv - 1)),
                dma((parts, n_shot - 1)),
                dma((parts, n_shot - 1)),
                dma((n_rcv - 1,)),
                dma((n_rcv - 1,)),
                dma((n_shot - 1,)),
                dma((n_shot - 1,)),
                dma((n_rcv - 1,)),
                dma((n_rcv - 1,)),
                dma((n_shot - 1,)),
                dma((n_shot - 1,)),
            ],
            compiler_params=pltpu.CompilerParams(
                collective_id=0,
                has_side_effects=True,
                vmem_limit_bytes=min(60 * 1024 * 1024, (63 << 20) - modeled.size * 8),
            ),
        )(modeled, observed, coupling, mask, shot_order, line_of_slot, wavelet, damping[None, :])
        return pl.pallas_call(
            finish,
            out_shape=(
                jax.ShapeDtypeStruct(wavelet.shape, f32),
                jax.ShapeDtypeStruct(modeled.shape, bf16),
            ),
            in_specs=[vmem] * 3,
            out_specs=(vmem, vmem),
            compiler_params=pltpu.CompilerParams(vmem_limit_bytes=modeled.size * 16 + (1 << 21)),
        )(*(pltpu.with_memory_space_constraint(x, pltpu.VMEM) for x in (new, wg, wdl)))

    placed = (
        P(None, "shot", None, "rcv", None),
        P(None, "shot", "rcv", None, None),
        P("shot", None, "rcv"),
        P(),
        P(),
        P(),
        P(),
        P(),
    )
    return jax.shard_map(
        per_device,
        mesh=mesh,
        in_specs=placed,
        out_specs=(P(), P(None, "shot", None, "rcv", None)),
        check_vma=False,
    )
```

```python
import functools

import jax
import jax.numpy as jnp
from jax import lax
from jax.experimental import pallas as pl
from jax.experimental.pallas import tpu as pltpu
from jax.sharding import PartitionSpec as P

MESH = pl.DeviceIdType.MESH
HBM = pltpu.MemorySpace.HBM
PIECES = 2


def peers_of(me, n):
    if n & (n - 1):
        return [lax.rem(me + d, n) for d in range(1, n)]
    out = []
    for j in range(1, n):
        peer, bit = me, 1
        while bit < n:
            if j & bit:
                peer = peer + bit * (1 - 2 * lax.rem(me // bit, 2))
            bit *= 2
        out.append(peer)
    return out


def kernel(
    n_shot,
    n_rcv,
    modeled_hbm,
    observed_hbm,
    coupling_hbm,
    mask_hbm,
    order_hbm,
    slot_hbm,
    wavelet_hbm,
    damping_hbm,
    new_ref,
    wg,
    wdl,
    mask_ref,
    order_ref,
    slot_ref,
    wavelet_ref,
    damping_ref,
    mod,
    obs,
    coup,
    spread,
    grouped,
    arrived,
    wd,
    live,
    num_mine,
    num_rcv,
    num_group,
    num_shot,
    den_mine,
    den_rcv,
    den_group,
    den_shot,
    load_sem,
    own_sem,
    send1,
    recv1,
    send2,
    recv2,
    num_send1,
    num_recv1,
    num_send2,
    num_recv2,
    den_send1,
    den_recv1,
    den_send2,
    den_recv2,
):
    me_s = lax.axis_index("shot")
    me_r = lax.axis_index("rcv")
    size, lines, rows, freqs = modeled_hbm.shape[1:]
    held = observed_hbm.shape[2]
    parts = len(spread)
    width = spread[0].shape[2]

    rcv_peers = peers_of(me_r, n_rcv)
    shot_peers = peers_of(me_s, n_shot)

    barrier = pltpu.get_barrier_semaphore()
    for r in rcv_peers:
        pl.semaphore_signal(barrier, inc=1, device_id=(me_s, r), device_id_type=MESH)
    for s in shot_peers:
        pl.semaphore_signal(barrier, inc=1, device_id=(s, me_r), device_id_type=MESH)

    small = [
        pltpu.make_async_copy(src, dst, load_sem.at[2 + i])
        for i, (src, dst) in enumerate(
            (
                (mask_hbm, mask_ref),
                (order_hbm, order_ref),
                (slot_hbm, slot_ref),
                (wavelet_hbm, wavelet_ref),
                (damping_hbm, damping_ref),
            )
        )
    ]
    for copy in small:
        copy.start()
    load_obs = pltpu.make_async_copy(observed_hbm, obs, load_sem.at[7])
    load_obs.start()
    load_mod = pltpu.make_async_copy(modeled_hbm, mod, load_sem.at[0])
    load_coup = pltpu.make_async_copy(coupling_hbm, coup, load_sem.at[1])
    load_mod.start()
    load_coup.start()

    def piece(t, r):
        c, h = divmod(t, parts // 2)
        return obs.at[
            c, 0, :, pl.ds(pl.multiple_of(r * rows, rows), rows), pl.ds(h * width, width)
        ]

    load_obs.wait()
    own = []
    for t in range(parts):
        copy = pltpu.make_async_copy(
            piece(t, me_r), spread[t].at[pl.ds(me_r * held, held)], own_sem.at[t]
        )
        copy.start()
        own.append(copy)

    pl.semaphore_wait(barrier, n_rcv + n_shot - 2)

    def spread_copy(t, d):
        return pltpu.make_async_remote_copy(
            src_ref=piece(t, rcv_peers[d - 1]),
            dst_ref=spread[t].at[pl.ds(me_r * held, held)],
            send_sem=send1.at[t, d - 1],
            recv_sem=recv1.at[t, d - 1],
            device_id=(me_s, rcv_peers[d - 1]),
            device_id_type=MESH,
        )

    def group_copy(t, d):
        return pltpu.make_async_remote_copy(
            src_ref=grouped.at[t, d - 1],
            dst_ref=arrived.at[t, me_s],
            send_sem=send2.at[t, d - 1],
            recv_sem=recv2.at[t, d - 1],
            device_id=(shot_peers[d - 1], me_r),
            device_id_type=MESH,
        )

    def rcv_sum(mine, slots, send, recv, start):
        for d in range(1, n_rcv):
            copy = pltpu.make_async_remote_copy(
                src_ref=mine,
                dst_ref=slots.at[me_r],
                send_sem=send.at[d - 1],
                recv_sem=recv.at[d - 1],
                device_id=(me_s, rcv_peers[d - 1]),
                device_id_type=MESH,
            )
            if start:
                copy.start()
            else:
                copy.wait()

    def shot_sum(mine, slots, send, recv, start):
        for d in range(1, n_shot):
            copy = pltpu.make_async_remote_copy(
                src_ref=mine,
                dst_ref=slots.at[me_s],
                send_sem=send.at[d - 1],
                recv_sem=recv.at[d - 1],
                device_id=(shot_peers[d - 1], me_r),
                device_id_type=MESH,
            )
            if start:
                copy.start()
            else:
                copy.wait()

    def total(slots, count):
        out = slots[0]
        for i in range(1, count):
            out = out + slots[i]
        return out

    for t in range(parts):
        for d in range(1, n_rcv):
            spread_copy(t, d).start()

    for copy in small:
        copy.wait()

    eye = (
        lax.broadcasted_iota(jnp.int32, (rows, rows), 0)
        == lax.broadcasted_iota(jnp.int32, (rows, rows), 1)
    )
    for p in range(size):
        for l in range(lines):
            flags = jnp.broadcast_to(mask_ref[p, l : l + 1, :].astype(jnp.float32), (rows, rows))
            column = jnp.sum(jnp.where(eye, flags, 0.0), axis=1, keepdims=True)
            live[p * lines + l] = jnp.broadcast_to(column, (rows, live.shape[2]))

    load_mod.wait()
    load_coup.wait()

    def dot(x, c):
        return jnp.dot(x, c, preferred_element_type=jnp.float32)

    tall = size * lines * rows
    x_re = mod[0].reshape(tall, freqs)
    x_im = mod[1].reshape(tall, freqs)
    wide = freqs // live.shape[2]

    def live_of(i):
        flag = live[i]
        return jnp.concatenate([flag] * wide, axis=1)

    wg[0] = (dot(x_re, coup[0]) - dot(x_im, coup[1])).reshape(size * lines, rows, freqs)
    wg[1] = (dot(x_re, coup[1]) + dot(x_im, coup[0])).reshape(size * lines, rows, freqs)

    den = jnp.zeros((rows, freqs), jnp.float32)
    for i in range(size * lines):
        flag = live_of(i)
        g_re, g_im = flag * wg[0, i], flag * wg[1, i]
        wg[0, i] = g_re
        wg[1, i] = g_im
        den = den + (g_re * g_re + g_im * g_im)
    den_mine[...] = jnp.sum(den, axis=0, keepdims=True)
    den_rcv[me_r] = den_mine[...]
    rcv_sum(den_mine, den_rcv, den_send1, den_recv1, True)

    def multiply(t):
        c, h = divmod(t, parts // 2)
        for d in range(1, n_shot):
            group_copy(t, d).wait_recv()
        x = arrived[t].reshape(n_shot * size * rows, width)
        span = slice(h * width, (h + 1) * width)
        if c == 0:
            re = dot(x, coup[0, span, :]).reshape(n_shot, size * rows, freqs)
            im = dot(x, coup[1, span, :]).reshape(n_shot, size * rows, freqs)
        else:
            re = -dot(x, coup[1, span, :]).reshape(n_shot, size * rows, freqs)
            im = dot(x, coup[0, span, :]).reshape(n_shot, size * rows, freqs)
        if t == 0:
            wd[0] = re
            wd[1] = im
        else:
            wd[0] = wd[0] + re
            wd[1] = wd[1] + im

    for t in range(parts):
        own[t].wait()
        for d in range(1, n_rcv):
            spread_copy(t, d).wait_recv()
        for d in list(range(1, n_shot)) + [0]:
            if d == 0:
                for e in range(1, n_shot):
                    group_copy(t, e).start()
            group = shot_peers[d - 1] if d else me_s
            for p in range(0, size, 2):
                first = order_ref[group * size + p]
                second = order_ref[group * size + p + 1]
                pair = jnp.concatenate([spread[t][first], spread[t][second]], axis=0)
                if d:
                    grouped[t, d - 1, p * rows : (p + 2) * rows, :] = pair
                else:
                    arrived[t, me_s, p * rows : (p + 2) * rows, :] = pair
        if t == parts - 1:
            rcv_sum(den_mine, den_rcv, den_send1, den_recv1, False)
            den_group[...] = total(den_rcv, n_rcv)
            den_shot[me_s] = den_group[...]
            shot_sum(den_group, den_shot, den_send2, den_recv2, True)
        if t > 0:
            multiply(t - 1)
    multiply(parts - 1)

    slot_of = []
    for l in range(lines):
        k = jnp.int32(0)
        for j in range(lines):
            k = jnp.where(slot_ref[j] == l, j, k)
        slot_of.append(k)

    w_re, w_im = wavelet_ref[0:1, :], wavelet_ref[1:2, :]
    num_re = jnp.zeros((rows, freqs), jnp.float32)
    num_im = jnp.zeros((rows, freqs), jnp.float32)
    for l in range(lines):
        for p in range(size):
            i = p * lines + l
            g_re, g_im, flag = wg[0, i], wg[1, i], live_of(i)
            at = slice(p * rows, (p + 1) * rows)
            d_re = flag * wd[0, slot_of[l], at, :]
            d_im = flag * wd[1, slot_of[l], at, :]
            wdl[0, i] = d_re
            wdl[1, i] = d_im
            res_re = d_re - (w_re * g_re - w_im * g_im)
            res_im = d_im - (w_re * g_im + w_im * g_re)
            num_re = num_re + (g_re * res_re + g_im * res_im)
            num_im = num_im + (g_re * res_im - g_im * res_re)
    num_mine[0:1, :] = jnp.sum(num_re, axis=0, keepdims=True)
    num_mine[1:2, :] = jnp.sum(num_im, axis=0, keepdims=True)
    num_rcv[me_r] = num_mine[...]
    rcv_sum(num_mine, num_rcv, num_send1, num_recv1, True)
    rcv_sum(num_mine, num_rcv, num_send1, num_recv1, False)
    num_group[...] = total(num_rcv, n_rcv)
    num_shot[me_s] = num_group[...]
    shot_sum(num_group, num_shot, num_send2, num_recv2, True)
    shot_sum(den_group, den_shot, den_send2, den_recv2, False)
    shot_sum(num_group, num_shot, num_send2, num_recv2, False)
    scale = total(den_shot, n_shot) + damping_ref[...]
    new = wavelet_ref[...] + total(num_shot, n_shot) / scale
    new_ref[...] = new

    for t in range(parts):
        for d in range(1, n_rcv):
            spread_copy(t, d).wait_send()
        for d in range(1, n_shot):
            group_copy(t, d).wait_send()


def finish(new_ref, wg, wdl, wave_out, out_ref):
    lines = out_ref.shape[2]
    wave_out[...] = new_ref[...]
    n_re, n_im = new_ref[0:1, :], new_ref[1:2, :]
    for i in range(wg.shape[1]):
        g_re, g_im = wg[0, i], wg[1, i]
        p, l = divmod(i, lines)
        out_ref[0, p, l] = (wdl[0, i] - (n_re * g_re - n_im * g_im)).astype(jnp.bfloat16)
        out_ref[1, p, l] = (wdl[1, i] - (n_re * g_im + n_im * g_re)).astype(jnp.bfloat16)


def solution(mesh):
    n_shot, n_rcv = mesh.shape["shot"], mesh.shape["rcv"]

    def per_device(modeled, observed, mask, shot_order, line_of_slot, coupling, wavelet, damping):
        _, size, lines, rows, freqs = modeled.shape
        shots = shot_order.shape[0]
        parts = 2 * PIECES
        width = freqs // PIECES
        f32, bf16 = jnp.float32, jnp.bfloat16
        dma = pltpu.SemaphoreType.DMA
        hbm = pl.BlockSpec(memory_space=HBM)
        vmem = pl.BlockSpec(memory_space=pltpu.VMEM)
        new, wg, wdl = pl.pallas_call(
            functools.partial(kernel, n_shot, n_rcv),
            out_shape=(
                pltpu.VMEM(wavelet.shape, f32),
                pltpu.VMEM((2, size * lines, rows, freqs), f32),
                pltpu.VMEM((2, size * lines, rows, freqs), f32),
            ),
            in_specs=[hbm] * 8,
            out_specs=(vmem, vmem, vmem),
            scratch_shapes=[
                pltpu.VMEM(mask.shape, jnp.int32),
                pltpu.SMEM(shot_order.shape, jnp.int32),
                pltpu.SMEM(line_of_slot.shape, jnp.int32),
                pltpu.VMEM(wavelet.shape, f32),
                pltpu.VMEM((1, freqs), f32),
                pltpu.VMEM(modeled.shape, bf16),
                pltpu.VMEM(observed.shape, bf16),
                pltpu.VMEM(coupling.shape, bf16),
                [pltpu.VMEM((shots, rows, width), bf16)] * parts,
                pltpu.VMEM((parts, n_shot - 1, size * rows, width), bf16),
                pltpu.VMEM((parts, n_shot, size * rows, width), bf16),
                pltpu.VMEM((2, n_shot, size * rows, freqs), f32),
                pltpu.VMEM((size * lines, rows, 128), f32),
                pltpu.VMEM((2, freqs), f32),
                pltpu.VMEM((n_rcv, 2, freqs), f32),
                pltpu.VMEM((2, freqs), f32),
                pltpu.VMEM((n_shot, 2, freqs), f32),
                pltpu.VMEM((1, freqs), f32),
                pltpu.VMEM((n_rcv, 1, freqs), f32),
                pltpu.VMEM((1, freqs), f32),
                pltpu.VMEM((n_shot, 1, freqs), f32),
                dma((8,)),
                dma((parts,)),
                dma((parts, n_rcv - 1)),
                dma((parts, n_rcv - 1)),
                dma((parts, n_shot - 1)),
                dma((parts, n_shot - 1)),
                dma((n_rcv - 1,)),
                dma((n_rcv - 1,)),
                dma((n_shot - 1,)),
                dma((n_shot - 1,)),
                dma((n_rcv - 1,)),
                dma((n_rcv - 1,)),
                dma((n_shot - 1,)),
                dma((n_shot - 1,)),
            ],
            compiler_params=pltpu.CompilerParams(
                collective_id=0,
                has_side_effects=True,
                vmem_limit_bytes=min(60 * 1024 * 1024, (63 << 20) - modeled.size * 8),
            ),
        )(modeled, observed, coupling, mask, shot_order, line_of_slot, wavelet, damping[None, :])
        return pl.pallas_call(
            finish,
            out_shape=(
                jax.ShapeDtypeStruct(wavelet.shape, f32),
                jax.ShapeDtypeStruct(modeled.shape, bf16),
            ),
            in_specs=[vmem] * 3,
            out_specs=(vmem, vmem),
            compiler_params=pltpu.CompilerParams(vmem_limit_bytes=modeled.size * 16 + (1 << 21)),
        )(*(pltpu.with_memory_space_constraint(x, pltpu.VMEM) for x in (new, wg, wdl)))

    placed = (
        P(None, "shot", None, "rcv", None),
        P(None, "shot", "rcv", None, None),
        P("shot", None, "rcv"),
        P(),
        P(),
        P(),
        P(),
        P(),
    )
    return jax.shard_map(
        per_device,
        mesh=mesh,
        in_specs=placed,
        out_specs=(P(), P(None, "shot", None, "rcv", None)),
        check_vma=False,
    )
```
